32 devices in a mesh: dp: 4 (over y, x), vocab: 8 (over z, core).
Axes of the slice: x: 2, y: 2, z: 4, core: 2. Of those that a mesh axis runs over, the one named last changes fastest.
Arguments:
- hidden: bfloat16 [192, 4096], P(('dp', 'vocab')), may hold values from -240 to 240
- head_weight: bfloat16 [4096, 163840], P(None, ('dp', 'vocab')), may hold values from -0.40625 to 0.40625
- targets: int32 [192], P(('dp', 'vocab')), may hold values from 0 to 163839, as said below
- image_mask: int32 [192], P(('dp', 'vocab')), may hold values from 0 to 1
- lengths: int32 [4], replicated, may hold values from 12 to 48, as said below
- ref_logps: float32 [4], replicated, may hold values from -18 to -13
- pairing: int32 [4], replicated, may hold values from 0 to 3, each once
Outputs:
- grad_hidden: bfloat16 [192, 4096], P(('dp', 'vocab'))
- grad_head: bfloat16 [4096, 163840], P(None, ('dp', 'vocab'))
- mean_loss: float32 [], replicated
The draws below stay inside these ranges and needn't reach their ends.
Inputs may be any that keep to these rules, and one draw needn't show every extreme that they name: `targets`: each token's target lies in its modality's columns: at least 131072 where image_mask is 1, below it where image_mask is 0. `lengths`: some window is full.
All inputs are finite; a program needn't handle non-finite values.
Results may differ from the reference program's by a relative error of at most 0.0067.
Values may be sent and summed in bfloat16 or wider, within the bound.
A program may use at most 192 MiB of HBM per device.

```python
import jax
import jax.numpy as jnp

D = 4096
V = 163840
CODES = 32768
WIN = 48
GROUPS = 4
TOKENS = 192


def token_tables(key):
    image_key = jax.random.fold_in(key, 11)
    text_key = jax.random.fold_in(key, 12)
    code_key = jax.random.fold_in(key, 13)
    image_flags = (jax.random.randint(image_key, (TOKENS,), 0, 3) == 0).astype(jnp.int32)
    text_ids = jax.random.randint(text_key, (TOKENS,), 0, V - CODES)
    code_ids = jax.random.randint(code_key, (TOKENS,), V - CODES, V)
    return (image_flags, jnp.where(image_flags == 1, code_ids, text_ids).astype(jnp.int32))


def draw_targets(key, part):
    return token_tables(key)[1]


def draw_image_mask(key, part):
    return token_tables(key)[0]


def draw_lengths(key, part):
    raw_lengths = jax.random.randint(jax.random.fold_in(key, 31), (GROUPS,), WIN // 4, WIN + 1)
    order = jax.random.permutation(jax.random.fold_in(key, 32), GROUPS)
    full_slot = jnp.arange(GROUPS, dtype=jnp.int32) == order[0]
    return jnp.where(full_slot, WIN, raw_lengths).astype(jnp.int32)


def draw_hidden(key, part):
    values = jnp.clip(jax.random.normal(jax.random.fold_in(key, 21), (TOKENS, D), jnp.float32), -6.0, 6.0)
    return values.astype(jnp.bfloat16)


def draw_head_weight(key, part):
    column_scale = 3.0 * D ** (-0.5)
    noise = jnp.clip(jax.random.normal(jax.random.fold_in(key, 41), (D, V), jnp.float32), -4.0, 4.0)
    offset = jnp.clip(jax.random.normal(jax.random.fold_in(key, 42), (D, 1), jnp.float32), -3.0, 3.0)
    values = column_scale * noise + 1.5 * column_scale * offset
    return values.astype(jnp.bfloat16)


def setup_inputs(seed: int = 0) -> dict:
    key_of = jax.random.split(jax.random.key(seed), 8)
    hidden = draw_hidden(jax.random.fold_in(key_of[7], 71), 0)
    head_weight = draw_head_weight(jax.random.fold_in(key_of[7], 71), 0)
    targets = draw_targets(jax.random.fold_in(key_of[7], 71), 0)
    image_mask = draw_image_mask(jax.random.fold_in(key_of[7], 71), 0)
    lengths = draw_lengths(jax.random.fold_in(key_of[7], 71), 0)
    ref_logps = jnp.clip(jax.random.uniform(key_of[5], (GROUPS,), jnp.float32, -18.0, -13.0), -18.0, -13.0)
    pairing = jax.random.permutation(key_of[6], GROUPS).astype(jnp.int32)
    return {"hidden": hidden, "head_weight": head_weight, "targets": targets, "image_mask": image_mask, "lengths": lengths, "ref_logps": ref_logps, "pairing": pairing}


NEG = -1e30
BETA = 1.0
LOSS_SCALE = 4096.0


def preference(token_lp, lengths, ref_logps, pairing):
    groups = lengths.shape[0]
    per_group = token_lp.reshape(groups, WIN)
    is_valid = jnp.arange(WIN, dtype=jnp.int32)[None, :] < lengths[:, None]
    token_count = lengths.astype(jnp.float32)
    policy = jnp.sum(jnp.where(is_valid, per_group, 0.0), axis=1) / token_count
    shifted = policy - ref_logps
    members = jnp.arange(groups, dtype=jnp.int32)
    chosen = (pairing[0::2][:, None] == members[None, :]).astype(jnp.float32)
    rejected = (pairing[1::2][:, None] == members[None, :]).astype(jnp.float32)
    pair_signs = chosen - rejected
    margin = BETA * jnp.sum(pair_signs * shifted[None, :], axis=1)
    mean_loss = jnp.mean(jax.nn.softplus(-margin))
    pair_weight = -LOSS_SCALE * BETA * jax.nn.sigmoid(-margin) / margin.shape[0]
    group_weight = jnp.sum(pair_weight[:, None] * pair_signs, axis=0) / token_count
    token_weight = jnp.where(is_valid, group_weight[:, None], 0.0).reshape(-1)
    return mean_loss, token_weight


def reference(hidden, head_weight, targets, image_mask, lengths, ref_logps, pairing):
    logits = jnp.dot(hidden, head_weight, preferred_element_type=jnp.float32)
    column_ids = jnp.arange(V, dtype=jnp.int32)
    code_column = column_ids >= V - CODES
    in_range = (image_mask[:, None] == 1) == code_column[None, :]
    masked = jnp.where(in_range, logits, NEG)
    row_peak = jnp.max(masked, axis=1)
    row_total = jnp.sum(jnp.where(in_range, jnp.exp(masked - row_peak[:, None]), 0.0), axis=1)
    log_norm = row_peak + jnp.log(row_total)
    is_target = column_ids[None, :] == targets[:, None]
    target_logit = jnp.sum(jnp.where(is_target, logits, 0.0), axis=1)
    token_lp = target_logit - log_norm
    mean_loss, token_weight = preference(token_lp, lengths, ref_logps, pairing)
    row_probs = jnp.where(in_range, jnp.exp(logits - log_norm[:, None]), 0.0)
    logit_grad = (token_weight[:, None] * (is_target.astype(jnp.float32) - row_probs)).astype(jnp.bfloat16)
    grad_hidden = jnp.dot(logit_grad, head_weight.T, preferred_element_type=jnp.float32).astype(jnp.bfloat16)
    grad_head = jnp.dot(hidden.T, logit_grad, preferred_element_type=jnp.float32).astype(jnp.bfloat16)
    return grad_hidden, grad_head, mean_loss
```

```python
import functools

import jax
import jax.numpy as jnp
from jax import lax
from jax.experimental import pallas as pl
from jax.experimental.pallas import tpu as pltpu
from jax.sharding import PartitionSpec as P

V = 163840
CODES = 32768
WIN = 48

NEG = -1e30
BETA = 1.0
LOSS_SCALE = 4096.0

AG_CHUNKS = 4
AHEAD = 2
RS_PARTS = (3, 3, 1, 1)
LANES = 128
MESH = pl.DeviceIdType.MESH
F32 = jnp.float32
BF16 = jnp.bfloat16


def block_of(size, top):
    block = top
    while size % block:
        block -= LANES
    return block


def main_kernel(cfg, targets, lengths, ref_logps, pairing, hidden, w_hbm, gh, g_hbm, h_hbm, loss,
                w, hid, h, logits, g, gt, r1, tgt, norm_b, weight_b, packed, spread, sb1, rb1, sb2, rb2,
                s1, b1, acc, s2, b2, s3, b3,
                w_sem, a1s, a1r, a2s, a2r, a3s, a3r, t1s, t1r, t2s, t2r,
                c1s, c1r, c2s, c2r, c3s, c3r, out_sem):
    n_dp, n_v = cfg["n_dp"], cfg["n_v"]
    tokens, columns = g.shape
    half = w.shape[0] // 2
    wide = half + LANES
    rows = tokens // (n_dp * n_v)
    me = lax.axis_index("dp")
    mv = lax.axis_index("vocab")
    core = lax.rem(mv, 2)
    mate = mv + 1 - 2 * core
    peers = [lax.rem(mv + o, n_v) for o in range(1, n_v)]
    groups = [lax.rem(me + o, n_dp) for o in range(1, n_dp)]

    step = half // AG_CHUNKS
    spans = [(j * step, step) for j in range(AG_CHUNKS)]

    loads = []
    for j, (at, size) in enumerate(spans):
        for side in range(2):
            span = pl.ds(side * half + at, size)
            loads.append(pltpu.make_async_copy(w_hbm.at[span, :], w.at[span, :], w_sem.at[2 * j + side]))
            loads[-1].start()

    spot = lax.broadcasted_iota(jnp.int32, (8, LANES), 0)
    digit = lax.broadcasted_iota(jnp.int32, (8, LANES), 1)
    tail = jnp.zeros((8, LANES), F32)
    for r in range(rows):
        number = targets[r]
        high, middle, low = number // 65536, lax.rem(number // 256, 256), lax.rem(number, 256)
        value = jnp.where(digit == 0, high, jnp.where(digit == 1, middle, low)).astype(F32)
        tail = jnp.where(spot == r, value, tail)
    hid[...] = jnp.zeros_like(hid)
    for side in range(2):
        hid[0:rows, side * wide:side * wide + half] = hidden[:, side * half:side * half + half]
        hid[:, side * wide + half:side * wide + wide] = tail.astype(BF16)

    barrier = pltpu.get_barrier_semaphore()
    for v in peers:
        pl.semaphore_signal(barrier, inc=1, device_id=(me, v), device_id_type=MESH)
    for d in groups:
        pl.semaphore_signal(barrier, inc=1, device_id=(d, mv), device_id_type=MESH)
    pl.semaphore_wait(barrier, n_v - 1 + n_dp - 1)

    sent = []

    def send(src, dst, s_sem, r_sem, device):
        copy = pltpu.make_async_remote_copy(
            src_ref=src, dst_ref=dst, send_sem=s_sem, recv_sem=r_sem, device_id=device, device_id_type=MESH)
        copy.start()
        sent.append(copy)
        return copy

    def window(index):
        return pl.ds(pl.multiple_of(index * WIN, 16), WIN)

    padded = n_v * 8
    r_id = lax.broadcasted_iota(jnp.int32, (WIN, padded), 0)
    s_id = lax.broadcasted_iota(jnp.int32, (WIN, padded), 1)
    perm = jnp.zeros((WIN, padded), F32)
    for v in range(n_v):
        perm = jnp.where((s_id - 8 * v == r_id - rows * v) & (s_id >= 8 * v) & (s_id < 8 * v + rows), 1.0, perm)
    perm = perm.astype(BF16)

    def wire(j):
        at, size = spans[j]
        return at, size + (LANES if j == AG_CHUNKS - 1 else 0)

    first = {}

    def spread_rows(j):
        at, size = wire(j)
        copies = []
        for o, v in enumerate(peers):
            col = pl.multiple_of(lax.rem(v, 2) * wide + at, LANES)
            copies.append(send(hid.at[:, pl.ds(col, size)], r1.at[mv, :, pl.ds(at, size)],
                               a1s.at[j * n_v + o], a1r.at[j * n_v + o], (me, v)))
        first[j] = copies

    for j in range(min(AHEAD, AG_CHUNKS)):
        spread_rows(j)

    waiting = {}

    def mine(j):
        at, size = wire(j)
        return pl.ds(pl.multiple_of(core * wide + at, LANES), size)

    def gather_stage(j, k):
        at, size = wire(j)
        if k == 0:
            r1[mv, :, at:at + size] = hid[:, mine(j)]
            for copy in first[j]:
                copy.wait_recv()
            if j + AHEAD < AG_CHUNKS:
                spread_rows(j + AHEAD)
            block = r1[:, :, at:at + size].astype(F32).reshape(padded, size).astype(BF16)
            h[window(me), mine(j)] = jnp.dot(perm, block, preferred_element_type=F32).astype(BF16)
        else:
            for copy in waiting[j]:
                copy.wait_recv()
        if k == 0:
            ref = h.at[window(me), mine(j)]
            waiting[j] = [
                send(ref, ref, a2s.at[j * (n_dp - 1) + o], a2r.at[j * (n_dp - 1) + o], (d, mv))
                for o, d in enumerate(groups)
            ]
        elif k == 1:
            ref = h.at[:, mine(j)]
            waiting[j] = [send(ref, ref, a3s.at[j], a3r.at[j], (me, mate))]
        else:
            multiply(j)

    block = block_of(columns, 2560)
    first_column = (me * n_v + mv) * columns
    lane = lax.broadcasted_iota(jnp.int32, (tokens, LANES), 1)

    def ids(n):
        return (lane + (first_column + n * LANES)).astype(F32)

    def multiply(j):
        at, size = spans[j]
        loads[2 * j].wait()
        loads[2 * j + 1].wait()
        last = j == AG_CHUNKS - 1
        if last:
            digits = h[:, half:half + LANES].astype(F32)
            target = digits[:, 0:1] * 65536.0 + digits[:, 1:2] * 256.0 + digits[:, 2:3]
            tgt[...] = jnp.broadcast_to(target, (tokens, LANES))
            norm_b[...] = jnp.full((tokens, LANES), NEG, F32)

        def body(n, carry):
            start = pl.multiple_of(n * block, block)
            cols = pl.ds(start, block)
            part = jnp.dot(jnp.concatenate([h[:, at:at + size], h[:, wide + at:wide + at + size]], axis=1),
                           jnp.concatenate([w[at:at + size, cols], w[half + at:half + at + size, cols]], axis=0),
                           preferred_element_type=F32)
            if j > 0:
                part = logits[:, cols] + part
            if not last:
                logits[:, cols] = part
                return carry
            coded = tgt[...] >= V - CODES
            peak = norm_b[...]
            for i in range(block // LANES):
                shared = (lane + (first_column + start + i * LANES) >= V - CODES) == coded
                value = jnp.where(shared, part[:, i * LANES:(i + 1) * LANES], NEG)
                logits[:, pl.ds(pl.multiple_of(start + i * LANES, LANES), LANES)] = value
                peak = jnp.maximum(peak, value)
            norm_b[...] = peak
            return carry

        lax.fori_loop(0, columns // block, body, 0)

    for t in range(AG_CHUNKS + 2):
        for k in range(3):
            if 0 <= t - k < AG_CHUNKS:
                gather_stage(t - k, k)

    h_out = [
        pltpu.make_async_copy(h.at[:, pl.ds(side * wide, half)], h_hbm.at[:, pl.ds(side * half, half)],
                              out_sem.at[side])
        for side in range(2)
    ]
    for copy in h_out:
        copy.start()

    peak = jnp.max(norm_b[...], axis=1, keepdims=True)
    norm_b[...] = jnp.broadcast_to(peak, (tokens, LANES))
    strips = columns // LANES
    unroll = 5 if strips % 5 == 0 else 1

    def total_body(m, carry):
        total, hit = carry
        for i in range(unroll):
            n = m * unroll + i
            value = logits[:, pl.ds(pl.multiple_of(n * LANES, LANES), LANES)]
            total += jnp.exp(value - norm_b[...])
            hit += jnp.where(ids(n) == tgt[...], value, 0.0)
        return total, hit

    zero = jnp.zeros((tokens, LANES), F32)
    total, hit = lax.fori_loop(0, strips // unroll, total_body, (zero, zero))
    total = jnp.sum(total, axis=1, keepdims=True)
    hit = jnp.sum(hit, axis=1, keepdims=True)
    packed[...] = jnp.ones_like(packed)
    packed[0:tokens, :] = jnp.where(lane == 0, peak, jnp.where(lane == 1, total, hit))
    turned = packed[...].T
    lines = packed.shape[0] // LANES

    def pack(dst, parts):
        dst[...] = jnp.zeros_like(dst)
        for b in range(lines):
            for q, part in enumerate(parts):
                dst[3 * b + q:3 * b + q + 1, :] = part[:, b * LANES:(b + 1) * LANES]

    def combine(recv, n):
        tops, masses, values = [], [], []
        for b in range(lines):
            top = recv[0, 3 * b:3 * b + 1, :]
            for i in range(1, n):
                top = jnp.maximum(top, recv[i, 3 * b:3 * b + 1, :])
            mass = jnp.zeros_like(top)
            value = jnp.zeros_like(top)
            for i in range(n):
                mass += recv[i, 3 * b + 1:3 * b + 2, :] * jnp.exp(recv[i, 3 * b:3 * b + 1, :] - top)
                value += recv[i, 3 * b + 2:3 * b + 3, :]
            tops.append(top)
            masses.append(mass)
            values.append(value)
        return [jnp.concatenate(x, axis=1) for x in (tops, masses, values)]

    pack(sb1, [turned[0:1], turned[1:2], turned[2:3]])
    rb1[mv] = sb1[...]
    copies = [send(sb1, rb1.at[mv], t1s.at[o], t1r.at[o], (me, v)) for o, v in enumerate(peers)]
    for copy in copies:
        copy.wait_recv()
    pack(sb2, combine(rb1, n_v))
    rb2[me] = sb2[...]
    copies = [send(sb2, rb2.at[me], t2s.at[o], t2r.at[o], (d, mv)) for o, d in enumerate(groups)]
    for copy in copies:
        copy.wait_recv()
    top, mass, value = combine(rb2, n_dp)
    log_norm = top + jnp.log(mass)
    token_lp = value - log_norm

    n_groups = cfg["groups"]
    pairs = n_groups // 2
    token = lax.broadcasted_iota(jnp.int32, token_lp.shape, 1)
    live, shifted, counts = [], [], []
    for i in range(n_groups):
        live.append((token >= i * WIN) & (token < i * WIN + lengths[i]))
        counts.append(jnp.full((1, 1), lengths[i], jnp.int32).astype(F32))
        policy = jnp.sum(jnp.where(live[i], token_lp, 0.0), axis=1, keepdims=True) / counts[i]
        shifted.append(policy - ref_logps[i])
    weights = [jnp.zeros((1, 1), F32) for _ in range(n_groups)]
    loss_sum = jnp.zeros((1, 1), F32)
    for k in range(pairs):
        signs = [
            jnp.where(pairing[2 * k] == i, 1.0, 0.0) - jnp.where(pairing[2 * k + 1] == i, 1.0, 0.0)
            for i in range(n_groups)
        ]
        margin = jnp.zeros((1, 1), F32)
        for i in range(n_groups):
            margin += signs[i] * shifted[i]
        margin = BETA * margin
        small = jnp.exp(-jnp.abs(margin))
        loss_sum += jnp.maximum(-margin, 0.0) + jnp.log1p(small)
        sigmoid = jnp.where(margin >= 0.0, small, 1.0) / (1.0 + small)
        pair_weight = -LOSS_SCALE * BETA * sigmoid / pairs
        for i in range(n_groups):
            weights[i] += signs[i] * pair_weight
    loss[0, 0] = (loss_sum / pairs)[0, 0]
    weight = jnp.zeros_like(token_lp)
    for i in range(n_groups):
        weight = jnp.where(live[i], weights[i] / counts[i], weight)
    spread[...] = jnp.zeros_like(spread)
    spread[0:1, :] = log_norm
    spread[1:2, :] = weight
    columns_of = spread[...].T
    norm_b[...] = jnp.broadcast_to(columns_of[0:tokens, 0:1], (tokens, LANES))
    weight_b[...] = jnp.broadcast_to(columns_of[0:tokens, 1:2], (tokens, LANES))

    wide_strip = block_of(columns, 512)

    def grad_body(m, carry):
        start = pl.multiple_of(m * wide_strip, wide_strip)
        for i in range(wide_strip // LANES):
            cols = pl.ds(pl.multiple_of(start + i * LANES, LANES), LANES)
            prob = jnp.exp(logits[:, cols] - norm_b[...])
            here = jnp.where((lane + (first_column + start + i * LANES)).astype(F32) == tgt[...], 1.0, 0.0)
            g[:, cols] = (weight_b[...] * (here - prob)).astype(BF16)
        gt[pl.ds(start, wide_strip), :] = g[:, pl.ds(start, wide_strip)].T
        return carry

    lax.fori_loop(0, columns // wide_strip, grad_body, 0)
    g_out = pltpu.make_async_copy(g, g_hbm, out_sem.at[2])
    g_out.start()

    chunks = []
    at = 0
    for part in RS_PARTS:
        chunks.append((at, half * part // sum(RS_PARTS)))
        at += chunks[-1][1]

    def partial(row, span):
        rows_of_w = pl.ds(pl.multiple_of(row, LANES), span)
        return jnp.dot(w[rows_of_w, :], gt[...], preferred_element_type=F32).T

    pending = {}

    def compute(j):
        at, span = chunks[j]
        lanes = slice(at, at + span)
        s1[:, lanes] = partial((1 - core) * half + at, span).astype(BF16)
        copy = send(s1.at[:, pl.ds(at, span)], b1.at[:, pl.ds(at, span)], c1s.at[j], c1r.at[j], (me, mate))
        acc[:, :, lanes] = partial(core * half + at, span).reshape(n_dp, WIN, span)
        copy.wait_recv()
        acc[:, :, lanes] += b1[:, lanes].astype(F32).reshape(n_dp, WIN, span)
        for o, d in enumerate(groups):
            s2[o, :, lanes] = acc[d, :, lanes].astype(BF16)
        pending[j] = [
            send(s2.at[o, :, pl.ds(at, span)], b2.at[o, :, pl.ds(at, span)],
                 c2s.at[j * (n_dp - 1) + o], c2r.at[j * (n_dp - 1) + o], (d, mv))
            for o, d in enumerate(groups)
        ]

    def across(j):
        at, span = chunks[j]
        lanes = slice(at, at + span)
        for copy in pending[j]:
            copy.wait_recv()
        value = acc[me, :, lanes]
        for o in range(n_dp - 1):
            value += b2[o, :, lanes].astype(F32)
        mixed = lax.dot_general(perm, value.astype(BF16), (((0,), (0,)), ((), ())), preferred_element_type=F32)
        s3[:, :, lanes] = mixed.reshape(n_v, 8, span).astype(BF16)
        b3[mv, :, lanes] = s3[mv, :, lanes]
        pending[j] = [
            send(s3.at[v, :, pl.ds(at, span)], b3.at[mv, :, pl.ds(at, span)],
                 c3s.at[j * n_v + o], c3r.at[j * n_v + o], (me, v))
            for o, v in enumerate(peers)
        ]

    def finish(j):
        at, span = chunks[j]
        lanes = slice(at, at + span)
        for copy in pending[j]:
            copy.wait_recv()
        for side in range(2):
            value = b3[side, :, lanes].astype(F32)
            for v in range(side + 2, n_v, 2):
                value += b3[v, :, lanes].astype(F32)
            gh[:, side * half + at:side * half + at + span] = value[0:rows].astype(BF16)

    n_chunks = len(chunks)
    for t in range(n_chunks + 2):
        if t < n_chunks:
            compute(t)
        if 0 <= t - 1 < n_chunks:
            across(t - 1)
        if 0 <= t - 2 < n_chunks:
            finish(t - 2)

    for copy in sent:
        copy.wait_send()
    for copy in h_out:
        copy.wait()
    g_out.wait()


def head_kernel(rc, nb, slots, gh_hbm, h_hbm, g_hbm, gh_out, out, h, g, turned, buf, load_sem, out_sem, gh_sem):
    depth, columns = out.shape
    n_rows, n_cols = depth // rc, columns // nb
    passed = pltpu.make_async_copy(gh_hbm, gh_out, gh_sem)
    h_in, g_in = [], []
    for r in range(2 * n_rows):
        span = pl.ds(r * rc // 2, rc // 2)
        h_in.append(pltpu.make_async_copy(h_hbm.at[:, span], h.at[:, span], load_sem.at[r]))
    for c in range(n_cols):
        span = pl.ds(c * nb, nb)
        g_in.append(pltpu.make_async_copy(g_hbm.at[:, span], g.at[:, span], load_sem.at[2 * n_rows + c]))
    h_in[0].start()
    g_in[0].start()
    for copy in h_in[1:] + g_in[1:]:
        copy.start()
    passed.start()
    busy = {}
    used = 0
    for c in range(n_cols):
        cols = slice(c * nb, (c + 1) * nb)
        for r in range(n_rows):
            span = slice(r * rc, (r + 1) * rc)
            if c == 0:
                for q in range(2 * r, 2 * r + 2):
                    h_in[q].wait()
                    piece = slice(q * rc // 2, (q + 1) * rc // 2)
                    turned[piece, :] = h[:, piece].T
            if r == 0:
                g_in[c].wait()
            slot = used % slots
            used += 1
            if slot in busy:
                busy[slot].wait()
            buf[slot] = jnp.dot(turned[span, :], g[:, cols], preferred_element_type=F32).astype(BF16)
            busy[slot] = pltpu.make_async_copy(buf.at[slot], out.at[pl.ds(r * rc, rc), pl.ds(c * nb, nb)],
                                               out_sem.at[slot])
            busy[slot].start()
    for copy in busy.values():
        copy.wait()
    passed.wait()


def local(n_dp, n_v, hidden, head_weight, targets, image_mask, lengths, ref_logps, pairing):
    rows, depth = hidden.shape
    columns = head_weight.shape[1]
    tokens = rows * n_dp * n_v
    half = depth // 2
    wide = half + LANES
    tp = -(-tokens // LANES) * LANES
    lines = -(-3 * (tp // LANES) // 8) * 8
    dma = lambda n: pltpu.SemaphoreType.DMA((n,))
    smem = pl.BlockSpec(memory_space=pltpu.SMEM)
    vmem = pl.BlockSpec(memory_space=pltpu.VMEM)
    hbm = pl.BlockSpec(memory_space=pl.ANY)
    cfg = {"n_dp": n_dp, "n_v": n_v, "groups": lengths.shape[0]}
    grad_hidden, g, h, loss = pl.pallas_call(
        functools.partial(main_kernel, cfg),
        out_shape=(
            jax.ShapeDtypeStruct((rows, depth), BF16),
            jax.ShapeDtypeStruct((tokens, columns), BF16),
            jax.ShapeDtypeStruct((tokens, depth), BF16),
            jax.ShapeDtypeStruct((1, 1), F32),
        ),
        in_specs=[smem, smem, smem, smem, vmem, hbm],
        out_specs=(vmem, hbm, hbm, smem),
        scratch_shapes=[
            pltpu.VMEM((depth, columns), BF16),
            pltpu.VMEM((8, 2 * wide), BF16),
            pltpu.VMEM((tokens, 2 * wide), BF16),
            pltpu.VMEM((tokens, columns), F32),
            pltpu.VMEM((tokens, columns), BF16),
            pltpu.VMEM((columns, tokens), BF16),
            pltpu.VMEM((n_v, 8, wide), BF16),
            pltpu.VMEM((tokens, LANES), F32),
            pltpu.VMEM((tokens, LANES), F32),
            pltpu.VMEM((tokens, LANES), F32),
            pltpu.VMEM((tp, LANES), F32),
            pltpu.VMEM((LANES, tp), F32),
            pltpu.VMEM((lines, LANES), F32),
            pltpu.VMEM((n_v, lines, LANES), F32),
            pltpu.VMEM((lines, LANES), F32),
            pltpu.VMEM((n_dp, lines, LANES), F32),
            pltpu.VMEM((tokens, half), BF16),
            pltpu.VMEM((tokens, half), BF16),
            pltpu.VMEM((n_dp, WIN, half), F32),
            pltpu.VMEM((n_dp - 1, WIN, half), BF16),
            pltpu.VMEM((n_dp - 1, WIN, half), BF16),
            pltpu.VMEM((n_v, 8, half), BF16),
            pltpu.VMEM((n_v, 8, half), BF16),
            dma(2 * AG_CHUNKS),
            dma(AG_CHUNKS * n_v), dma(AG_CHUNKS * n_v),
            dma(AG_CHUNKS * (n_dp - 1)), dma(AG_CHUNKS * (n_dp - 1)),
            dma(AG_CHUNKS), dma(AG_CHUNKS),
            dma(n_v), dma(n_v), dma(n_dp), dma(n_dp),
            dma(len(RS_PARTS)), dma(len(RS_PARTS)),
            dma(len(RS_PARTS) * (n_dp - 1)), dma(len(RS_PARTS) * (n_dp - 1)),
            dma(len(RS_PARTS) * n_v), dma(len(RS_PARTS) * n_v),
            dma(3),
        ],
        compiler_params=pltpu.CompilerParams(
            collective_id=0, has_side_effects=True, vmem_limit_bytes=67_000_000
        ),
        name="loss_and_hidden_gradient",
    )(targets, lengths, ref_logps, pairing, hidden, head_weight)
    rc, nb, slots = depth // 2, block_of(columns, 1024), 3
    grad_hidden, grad_head = pl.pallas_call(
        functools.partial(head_kernel, rc, nb, slots),
        out_shape=(jax.ShapeDtypeStruct((rows, depth), BF16), jax.ShapeDtypeStruct((depth, columns), BF16)),
        in_specs=[hbm, hbm, hbm],
        out_specs=(hbm, hbm),
        scratch_shapes=[
            pltpu.VMEM((tokens, depth), BF16),
            pltpu.VMEM((tokens, columns), BF16),
            pltpu.VMEM((depth, tokens), BF16),
            pltpu.VMEM((slots, rc, nb), BF16),
            dma(4 + columns // nb), dma(slots), pltpu.SemaphoreType.DMA,
        ],
        compiler_params=pltpu.CompilerParams(vmem_limit_bytes=67_000_000),
        name="head_gradient",
    )(grad_hidden, h, g)
    return grad_hidden, grad_head, loss.reshape(())


def solution(mesh):
    return jax.shard_map(
        functools.partial(local, mesh.shape["dp"], mesh.shape["vocab"]),
        mesh=mesh,
        in_specs=(
            P(("dp", "vocab"), None),
            P(None, ("dp", "vocab")),
            P(("dp", "vocab")),
            P(("dp", "vocab")),
            P(),
            P(),
            P(),
        ),
        out_specs=(P(("dp", "vocab"), None), P(None, ("dp", "vocab")), P()),
        check_vma=False,
    )
```

```python
import functools

import jax
import jax.numpy as jnp
from jax import lax
from jax.experimental import pallas as pl
from jax.experimental.pallas import tpu as pltpu
from jax.sharding import PartitionSpec as P

V = 163840
CODES = 32768
WIN = 48

NEG = -1e30
BETA = 1.0
LOSS_SCALE = 4096.0

AG_CHUNKS = 4
AHEAD = 2
RS_PARTS = (3, 3, 1, 1)
LANES = 128
MESH = pl.DeviceIdType.MESH
F32 = jnp.float32
BF16 = jnp.bfloat16


def block_of(size, top):
    block = top
    while size % block:
        block -= LANES
    return block


def main_kernel(cfg, targets, lengths, ref_logps, pairing, hidden, w_hbm, gh, g_hbm, h_hbm, loss,
                w, hid, h, logits, g, gt, r1, tgt, norm_b, weight_b, packed, spread, sb1, rb1, sb2, rb2,
                s1, b1, acc, s2, b2, s3, b3,
                w_sem, a1s, a1r, a2s, a2r, a3s, a3r, t1s, t1r, t2s, t2r,
                c1s, c1r, c2s, c2r, c3s, c3r, out_sem):
    n_dp, n_v = cfg["n_dp"], cfg["n_v"]
    tokens, columns = g.shape
    half = w.shape[0] // 2
    wide = half + LANES
    rows = tokens // (n_dp * n_v)
    me = lax.axis_index("dp")
    mv = lax.axis_index("vocab")
    core = lax.rem(mv, 2)
    mate = mv + 1 - 2 * core
    peers = [lax.rem(mv + o, n_v) for o in range(1, n_v)]
    groups = [lax.rem(me + o, n_dp) for o in range(1, n_dp)]

    step = half // AG_CHUNKS
    spans = [(j * step, step) for j in range(AG_CHUNKS)]

    loads = []
    for j, (at, size) in enumerate(spans):
        for side in range(2):
            span = pl.ds(side * half + at, size)
            loads.append(pltpu.make_async_copy(w_hbm.at[span, :], w.at[span, :], w_sem.at[2 * j + side]))
            loads[-1].start()

    spot = lax.broadcasted_iota(jnp.int32, (8, LANES), 0)
    digit = lax.broadcasted_iota(jnp.int32, (8, LANES), 1)
    tail = jnp.zeros((8, LANES), F32)
    for r in range(rows):
        number = targets[r]
        high, middle, low = number // 65536, lax.rem(number // 256, 256), lax.rem(number, 256)
        value = jnp.where(digit == 0, high, jnp.where(digit == 1, middle, low)).astype(F32)
        tail = jnp.where(spot == r, value, tail)
    hid[...] = jnp.zeros_like(hid)
    for side in range(2):
        hid[0:rows, side * wide:side * wide + half] = hidden[:, side * half:side * half + half]
        hid[:, side * wide + half:side * wide + wide] = tail.astype(BF16)

    barrier = pltpu.get_barrier_semaphore()
    for v in peers:
        pl.semaphore_signal(barrier, inc=1, device_id=(me, v), device_id_type=MESH)
    for d in groups:
        pl.semaphore_signal(barrier, inc=1, device_id=(d, mv), device_id_type=MESH)
    pl.semaphore_wait(barrier, n_v - 1 + n_dp - 1)

    sent = []

    def send(src, dst, s_sem, r_sem, device):
        copy = pltpu.make_async_remote_copy(
            src_ref=src, dst_ref=dst, send_sem=s_sem, recv_sem=r_sem, device_id=device, device_id_type=MESH)
        copy.start()
        sent.append(copy)
        return copy

    def window(index):
        return pl.ds(pl.multiple_of(index * WIN, 16), WIN)

    padded = n_v * 8
    r_id = lax.broadcasted_iota(jnp.int32, (WIN, padded), 0)
    s_id = lax.broadcasted_iota(jnp.int32, (WIN, padded), 1)
    perm = jnp.zeros((WIN, padded), F32)
    for v in range(n_v):
        perm = jnp.where((s_id - 8 * v == r_id - rows * v) & (s_id >= 8 * v) & (s_id < 8 * v + rows), 1.0, perm)
    perm = perm.astype(BF16)

    def wire(j):
        at, size = spans[j]
        return at, size + (LANES if j == AG_CHUNKS - 1 else 0)

    first = {}

    def spread_rows(j):
        at, size = wire(j)
        copies = []
        for o, v in enumerate(peers):
            col = pl.multiple_of(lax.rem(v, 2) * wide + at, LANES)
            copies.append(send(hid.at[:, pl.ds(col, size)], r1.at[mv, :, pl.ds(at, size)],
                               a1s.at[j * n_v + o], a1r.at[j * n_v + o], (me, v)))
        first[j] = copies

    for j in range(min(AHEAD, AG_CHUNKS)):
        spread_rows(j)

    waiting = {}

    def mine(j):
        at, size = wire(j)
        return pl.ds(pl.multiple_of(core * wide + at, LANES), size)

    def gather_stage(j, k):
        at, size = wire(j)
        if k == 0:
            r1[mv, :, at:at + size] = hid[:, mine(j)]
            for copy in first[j]:
                copy.wait_recv()
            if j + AHEAD < AG_CHUNKS:
                spread_rows(j + AHEAD)
            block = r1[:, :, at:at + size].astype(F32).reshape(padded, size).astype(BF16)
            h[window(me), mine(j)] = jnp.dot(perm, block, preferred_element_type=F32).astype(BF16)
        else:
            for copy in waiting[j]:
                copy.wait_recv()
        if k == 0:
            ref = h.at[window(me), mine(j)]
            waiting[j] = [
                send(ref, ref, a2s.at[j * (n_dp - 1) + o], a2r.at[j * (n_dp - 1) + o], (d, mv))
                for o, d in enumerate(groups)
            ]
        elif k == 1:
            ref = h.at[:, mine(j)]
            waiting[j] = [send(ref, ref, a3s.at[j], a3r.at[j], (me, mate))]
        else:
            multiply(j)

    block = block_of(columns, 2560)
    first_column = (me * n_v + mv) * columns
    lane = lax.broadcasted_iota(jnp.int32, (tokens, LANES), 1)

    def ids(n):
        return (lane + (first_column + n * LANES)).astype(F32)

    def multiply(j):
        at, size = spans[j]
        loads[2 * j].wait()
        loads[2 * j + 1].wait()
        last = j == AG_CHUNKS - 1
        if last:
            digits = h[:, half:half + LANES].astype(F32)
            target = digits[:, 0:1] * 65536.0 + digits[:, 1:2] * 256.0 + digits[:, 2:3]
            tgt[...] = jnp.broadcast_to(target, (tokens, LANES))
            norm_b[...] = jnp.full((tokens, LANES), NEG, F32)

        def body(n, carry):
            start = pl.multiple_of(n * block, block)
            cols = pl.ds(start, block)
            part = jnp.dot(jnp.concatenate([h[:, at:at + size], h[:, wide + at:wide + at + size]], axis=1),
                           jnp.concatenate([w[at:at + size, cols], w[half + at:half + at + size, cols]], axis=0),
                           preferred_element_type=F32)
            if j > 0:
                part = logits[:, cols] + part
            if not last:
                logits[:, cols] = part
                return carry
            coded = tgt[...] >= V - CODES
            peak = norm_b[...]
            for i in range(block // LANES):
                shared = (lane + (first_column + start + i * LANES) >= V - CODES) == coded
                value = jnp.where(shared, part[:, i * LANES:(i + 1) * LANES], NEG)
                logits[:, pl.ds(pl.multiple_of(start + i * LANES, LANES), LANES)] = value
                peak = jnp.maximum(peak, value)
            norm_b[...] = peak
            return carry

        lax.fori_loop(0, columns // block, body, 0)

    late = AG_CHUNKS - 1
    for t in range(AG_CHUNKS + 2):
        if t < late:
            gather_stage(t, 0)
        if 0 <= t - 1 < AG_CHUNKS:
            gather_stage(t - 1, 1)
        if t == late - 1:
            gather_stage(late, 0)
        if 0 <= t - 2 < AG_CHUNKS:
            gather_stage(t - 2, 2)

    h_out = [
        pltpu.make_async_copy(h.at[:, pl.ds(side * wide, half)], h_hbm.at[:, pl.ds(side * half, half)],
                              out_sem.at[side])
        for side in range(2)
    ]
    for copy in h_out:
        copy.start()

    peak = jnp.max(norm_b[...], axis=1, keepdims=True)
    norm_b[...] = jnp.broadcast_to(peak, (tokens, LANES))
    strips = columns // LANES
    unroll = 5 if strips % 5 == 0 else 1

    def total_body(m, carry):
        total, hit = carry
        for i in range(unroll):
            n = m * unroll + i
            value = logits[:, pl.ds(pl.multiple_of(n * LANES, LANES), LANES)]
            total += jnp.exp(value - norm_b[...])
            hit += jnp.where(ids(n) == tgt[...], value, 0.0)
        return total, hit

    zero = jnp.zeros((tokens, LANES), F32)
    total, hit = lax.fori_loop(0, strips // unroll, total_body, (zero, zero))
    total = jnp.sum(total, axis=1, keepdims=True)
    hit = jnp.sum(hit, axis=1, keepdims=True)
    packed[...] = jnp.ones_like(packed)
    packed[0:tokens, :] = jnp.where(lane == 0, peak, jnp.where(lane == 1, total, hit))
    turned = packed[...].T
    lines = packed.shape[0] // LANES

    def pack(dst, parts):
        dst[...] = jnp.zeros_like(dst)
        for b in range(lines):
            for q, part in enumerate(parts):
                dst[3 * b + q:3 * b + q + 1, :] = part[:, b * LANES:(b + 1) * LANES]

    def combine(recv, n):
        tops, masses, values = [], [], []
        for b in range(lines):
            top = recv[0, 3 * b:3 * b + 1, :]
            for i in range(1, n):
                top = jnp.maximum(top, recv[i, 3 * b:3 * b + 1, :])
            mass = jnp.zeros_like(top)
            value = jnp.zeros_like(top)
            for i in range(n):
                mass += recv[i, 3 * b + 1:3 * b + 2, :] * jnp.exp(recv[i, 3 * b:3 * b + 1, :] - top)
                value += recv[i, 3 * b + 2:3 * b + 3, :]
            tops.append(top)
            masses.append(mass)
            values.append(value)
        return [jnp.concatenate(x, axis=1) for x in (tops, masses, values)]

    pack(sb1, [turned[0:1], turned[1:2], turned[2:3]])
    rb1[mv] = sb1[...]
    copies = [send(sb1, rb1.at[mv], t1s.at[o], t1r.at[o], (me, v)) for o, v in enumerate(peers)]
    for copy in copies:
        copy.wait_recv()
    pack(sb2, combine(rb1, n_v))
    rb2[me] = sb2[...]
    copies = [send(sb2, rb2.at[me], t2s.at[o], t2r.at[o], (d, mv)) for o, d in enumerate(groups)]
    for copy in copies:
        copy.wait_recv()
    top, mass, value = combine(rb2, n_dp)
    log_norm = top + jnp.log(mass)
    token_lp = value - log_norm

    n_groups = cfg["groups"]
    pairs = n_groups // 2
    token = lax.broadcasted_iota(jnp.int32, token_lp.shape, 1)
    live, shifted, counts = [], [], []
    for i in range(n_groups):
        live.append((token >= i * WIN) & (token < i * WIN + lengths[i]))
        counts.append(jnp.full((1, 1), lengths[i], jnp.int32).astype(F32))
        policy = jnp.sum(jnp.where(live[i], token_lp, 0.0), axis=1, keepdims=True) / counts[i]
        shifted.append(policy - ref_logps[i])
    weights = [jnp.zeros((1, 1), F32) for _ in range(n_groups)]
    loss_sum = jnp.zeros((1, 1), F32)
    for k in range(pairs):
        signs = [
            jnp.where(pairing[2 * k] == i, 1.0, 0.0) - jnp.where(pairing[2 * k + 1] == i, 1.0, 0.0)
            for i in range(n_groups)
        ]
        margin = jnp.zeros((1, 1), F32)
        for i in range(n_groups):
            margin += signs[i] * shifted[i]
        margin = BETA * margin
        small = jnp.exp(-jnp.abs(margin))
        loss_sum += jnp.maximum(-margin, 0.0) + jnp.log1p(small)
        sigmoid = jnp.where(margin >= 0.0, small, 1.0) / (1.0 + small)
        pair_weight = -LOSS_SCALE * BETA * sigmoid / pairs
        for i in range(n_groups):
            weights[i] += signs[i] * pair_weight
    loss[0, 0] = (loss_sum / pairs)[0, 0]
    weight = jnp.zeros_like(token_lp)
    for i in range(n_groups):
        weight = jnp.where(live[i], weights[i] / counts[i], weight)
    spread[...] = jnp.zeros_like(spread)
    spread[0:1, :] = log_norm
    spread[1:2, :] = weight
    columns_of = spread[...].T
    norm_b[...] = jnp.broadcast_to(columns_of[0:tokens, 0:1], (tokens, LANES))
    weight_b[...] = jnp.broadcast_to(columns_of[0:tokens, 1:2], (tokens, LANES))

    wide_strip = block_of(columns, 512)

    def grad_body(m, carry):
        start = pl.multiple_of(m * wide_strip, wide_strip)
        for i in range(wide_strip // LANES):
            cols = pl.ds(pl.multiple_of(start + i * LANES, LANES), LANES)
            prob = jnp.exp(logits[:, cols] - norm_b[...])
            here = jnp.where((lane + (first_column + start + i * LANES)).astype(F32) == tgt[...], 1.0, 0.0)
            g[:, cols] = (weight_b[...] * (here - prob)).astype(BF16)
        gt[pl.ds(start, wide_strip), :] = g[:, pl.ds(start, wide_strip)].T
        return carry

    lax.fori_loop(0, columns // wide_strip, grad_body, 0)
    g_out = pltpu.make_async_copy(g, g_hbm, out_sem.at[2])
    g_out.start()

    chunks = []
    at = 0
    for part in RS_PARTS:
        chunks.append((at, half * part // sum(RS_PARTS)))
        at += chunks[-1][1]

    def partial(row, span):
        size = span // 2
        halves = []
        for i in range(2):
            rows_of_w = pl.ds(pl.multiple_of(row + i * size, LANES), size)
            halves.append(jnp.dot(w[rows_of_w, :], gt[...], preferred_element_type=F32))
        return jnp.concatenate([part.T for part in halves], axis=1)

    pending = {}

    def other(j):
        at, span = chunks[j]
        s1[:, at:at + span] = partial((1 - core) * half + at, span).astype(BF16)
        pending[j] = [send(s1.at[:, pl.ds(at, span)], b1.at[:, pl.ds(at, span)], c1s.at[j], c1r.at[j], (me, mate))]

    def own(j):
        at, span = chunks[j]
        acc[:, :, at:at + span] = partial(core * half + at, span).reshape(n_dp, WIN, span)

    def join(j):
        at, span = chunks[j]
        lanes = slice(at, at + span)
        for copy in pending[j]:
            copy.wait_recv()
        acc[:, :, lanes] += b1[:, lanes].astype(F32).reshape(n_dp, WIN, span)
        for o, d in enumerate(groups):
            s2[o, :, lanes] = acc[d, :, lanes].astype(BF16)
        pending[j] = [
            send(s2.at[o, :, pl.ds(at, span)], b2.at[o, :, pl.ds(at, span)],
                 c2s.at[j * (n_dp - 1) + o], c2r.at[j * (n_dp - 1) + o], (d, mv))
            for o, d in enumerate(groups)
        ]

    def across(j):
        at, span = chunks[j]
        lanes = slice(at, at + span)
        for copy in pending[j]:
            copy.wait_recv()
        value = acc[me, :, lanes]
        for o in range(n_dp - 1):
            value += b2[o, :, lanes].astype(F32)
        mixed = lax.dot_general(perm, value.astype(BF16), (((0,), (0,)), ((), ())), preferred_element_type=F32)
        s3[:, :, lanes] = mixed.reshape(n_v, 8, span).astype(BF16)
        b3[mv, :, lanes] = s3[mv, :, lanes]
        pending[j] = [
            send(s3.at[v, :, pl.ds(at, span)], b3.at[mv, :, pl.ds(at, span)],
                 c3s.at[j * n_v + o], c3r.at[j * n_v + o], (me, v))
            for o, v in enumerate(peers)
        ]

    def finish(j):
        at, span = chunks[j]
        lanes = slice(at, at + span)
        for copy in pending[j]:
            copy.wait_recv()
        for side in range(2):
            value = b3[side, :, lanes].astype(F32)
            for v in range(side + 2, n_v, 2):
                value += b3[v, :, lanes].astype(F32)
            gh[:, side * half + at:side * half + at + span] = value[0:rows].astype(BF16)

    n_chunks = len(chunks)
    other(0)
    for t in range(n_chunks + 2):
        if t + 1 < n_chunks:
            other(t + 1)
        if t < n_chunks - 1:
            own(t)
            join(t)
        if t == n_chunks - 2:
            own(t + 1)
            join(t + 1)
        if 0 <= t - 1 < n_chunks:
            across(t - 1)
        if 0 <= t - 2 < n_chunks:
            finish(t - 2)

    for copy in sent:
        copy.wait_send()
    for copy in h_out:
        copy.wait()
    g_out.wait()


def head_kernel(rc, nb, slots, gh_hbm, h_hbm, g_hbm, gh_out, out, h, g, turned, buf, load_sem, out_sem, gh_sem):
    depth, columns = out.shape
    n_rows, n_cols = depth // rc, columns // nb
    passed = pltpu.make_async_copy(gh_hbm, gh_out, gh_sem)
    h_in, g_in = [], []
    for r in range(2 * n_rows):
        span = pl.ds(r * rc // 2, rc // 2)
        h_in.append(pltpu.make_async_copy(h_hbm.at[:, span], h.at[:, span], load_sem.at[r]))
    for c in range(n_cols):
        span = pl.ds(c * nb, nb)
        g_in.append(pltpu.make_async_copy(g_hbm.at[:, span], g.at[:, span], load_sem.at[2 * n_rows + c]))
    h_in[0].start()
    g_in[0].start()
    for copy in h_in[1:] + g_in[1:]:
        copy.start()
    passed.start()
    busy = {}
    used = 0
    for c in range(n_cols):
        cols = slice(c * nb, (c + 1) * nb)
        for r in range(n_rows):
            span = slice(r * rc, (r + 1) * rc)
            if c == 0:
                for q in range(2 * r, 2 * r + 2):
                    h_in[q].wait()
                    piece = slice(q * rc // 2, (q + 1) * rc // 2)
                    turned[piece, :] = h[:, piece].T
            if r == 0:
                g_in[c].wait()
            slot = used % slots
            used += 1
            if slot in busy:
                busy[slot].wait()
            buf[slot] = jnp.dot(turned[span, :], g[:, cols], preferred_element_type=F32).astype(BF16)
            busy[slot] = pltpu.make_async_copy(buf.at[slot], out.at[pl.ds(r * rc, rc), pl.ds(c * nb, nb)],
                                               out_sem.at[slot])
            busy[slot].start()
    for copy in busy.values():
        copy.wait()
    passed.wait()


def local(n_dp, n_v, hidden, head_weight, targets, image_mask, lengths, ref_logps, pairing):
    rows, depth = hidden.shape
    columns = head_weight.shape[1]
    tokens = rows * n_dp * n_v
    half = depth // 2
    wide = half + LANES
    tp = -(-tokens // LANES) * LANES
    lines = -(-3 * (tp // LANES) // 8) * 8
    dma = lambda n: pltpu.SemaphoreType.DMA((n,))
    smem = pl.BlockSpec(memory_space=pltpu.SMEM)
    vmem = pl.BlockSpec(memory_space=pltpu.VMEM)
    hbm = pl.BlockSpec(memory_space=pl.ANY)
    cfg = {"n_dp": n_dp, "n_v": n_v, "groups": lengths.shape[0]}
    grad_hidden, g, h, loss = pl.pallas_call(
        functools.partial(main_kernel, cfg),
        out_shape=(
            jax.ShapeDtypeStruct((rows, depth), BF16),
            jax.ShapeDtypeStruct((tokens, columns), BF16),
            jax.ShapeDtypeStruct((tokens, depth), BF16),
            jax.ShapeDtypeStruct((1, 1), F32),
        ),
        in_specs=[smem, smem, smem, smem, vmem, hbm],
        out_specs=(vmem, hbm, hbm, smem),
        scratch_shapes=[
            pltpu.VMEM((depth, columns), BF16),
            pltpu.VMEM((8, 2 * wide), BF16),
            pltpu.VMEM((tokens, 2 * wide), BF16),
            pltpu.VMEM((tokens, columns), F32),
            pltpu.VMEM((tokens, columns), BF16),
            pltpu.VMEM((columns, tokens), BF16),
            pltpu.VMEM((n_v, 8, wide), BF16),
            pltpu.VMEM((tokens, LANES), F32),
            pltpu.VMEM((tokens, LANES), F32),
            pltpu.VMEM((tokens, LANES), F32),
            pltpu.VMEM((tp, LANES), F32),
            pltpu.VMEM((LANES, tp), F32),
            pltpu.VMEM((lines, LANES), F32),
            pltpu.VMEM((n_v, lines, LANES), F32),
            pltpu.VMEM((lines, LANES), F32),
            pltpu.VMEM((n_dp, lines, LANES), F32),
            pltpu.VMEM((tokens, half), BF16),
            pltpu.VMEM((tokens, half), BF16),
            pltpu.VMEM((n_dp, WIN, half), F32),
            pltpu.VMEM((n_dp - 1, WIN, half), BF16),
            pltpu.VMEM((n_dp - 1, WIN, half), BF16),
            pltpu.VMEM((n_v, 8, half), BF16),
            pltpu.VMEM((n_v, 8, half), BF16),
            dma(2 * AG_CHUNKS),
            dma(AG_CHUNKS * n_v), dma(AG_CHUNKS * n_v),
            dma(AG_CHUNKS * (n_dp - 1)), dma(AG_CHUNKS * (n_dp - 1)),
            dma(AG_CHUNKS), dma(AG_CHUNKS),
            dma(n_v), dma(n_v), dma(n_dp), dma(n_dp),
            dma(len(RS_PARTS)), dma(len(RS_PARTS)),
            dma(len(RS_PARTS) * (n_dp - 1)), dma(len(RS_PARTS) * (n_dp - 1)),
            dma(len(RS_PARTS) * n_v), dma(len(RS_PARTS) * n_v),
            dma(3),
        ],
        compiler_params=pltpu.CompilerParams(
            collective_id=0, has_side_effects=True, vmem_limit_bytes=67_000_000
        ),
        name="loss_and_hidden_gradient",
    )(targets, lengths, ref_logps, pairing, hidden, head_weight)
    rc, nb, slots = depth // 2, block_of(columns, 1024), 3
    grad_hidden, grad_head = pl.pallas_call(
        functools.partial(head_kernel, rc, nb, slots),
        out_shape=(jax.ShapeDtypeStruct((rows, depth), BF16), jax.ShapeDtypeStruct((depth, columns), BF16)),
        in_specs=[hbm, hbm, hbm],
        out_specs=(hbm, hbm),
        scratch_shapes=[
            pltpu.VMEM((tokens, depth), BF16),
            pltpu.VMEM((tokens, columns), BF16),
            pltpu.VMEM((depth, tokens), BF16),
            pltpu.VMEM((slots, rc, nb), BF16),
            dma(4 + columns // nb), dma(slots), pltpu.SemaphoreType.DMA,
        ],
        compiler_params=pltpu.CompilerParams(vmem_limit_bytes=67_000_000),
        name="head_gradient",
    )(grad_hidden, h, g)
    return grad_hidden, grad_head, loss.reshape(())


def solution(mesh):
    return jax.shard_map(
        functools.partial(local, mesh.shape["dp"], mesh.shape["vocab"]),
        mesh=mesh,
        in_specs=(
            P(("dp", "vocab"), None),
            P(None, ("dp", "vocab")),
            P(("dp", "vocab")),
            P(("dp", "vocab")),
            P(),
            P(),
            P(),
        ),
        out_specs=(P(("dp", "vocab"), None), P(None, ("dp", "vocab")), P()),
        check_vma=False,
    )
```
